32 devices in a mesh: parts: 16 (over z, y, core), mp: 2 (over x).
Axes of the slice: x: 2, y: 2, z: 4, core: 2. Of those that a mesh axis runs over, the one named last changes fastest.
Arguments:
- feats: bfloat16 [2048, 1024], P('parts', 'mp'), may hold values from -6 to 6
- adj_local: bfloat16 [2048, 128], P('parts'), may hold values from -0.5 to 0.5
- adj_halo: bfloat16 [2048, 128], P('parts'), may hold values from -0.5 to 0.5
- w_graph: bfloat16 [1024, 1024], P(None, 'mp'), may hold values from -0.1875 to 0.1875
- w_query: bfloat16 [1024, 1024], P(None, 'mp'), may hold values from -0.1875 to 0.1875
- w_key: bfloat16 [1024, 1024], P(None, 'mp'), may hold values from -0.1875 to 0.1875
- w_value: bfloat16 [1024, 1024], P(None, 'mp'), may hold values from -0.1875 to 0.1875
- send_rows: int32 [16, 16, 8], P('parts'), may hold values from 0 to 127
- send_count: int32 [16, 16], P('parts'), may hold values from 0 to 8
- live: int32 [16], P('parts'), may hold values from 64 to 128
Outputs:
- attended: float32 [2048, 1024], P('parts', 'mp')
- key_summary: float32 [1024, 1024], P('mp')
The draws below stay inside these ranges and needn't reach their ends.
All inputs are finite; a program needn't handle non-finite values.
Results may differ from the reference program's by a relative error of at most 0.0029.
The reference program's roundings to bfloat16 on the way count: a program that leaves them out, or rounds other values in their place, can miss the bound.
Values may be sent and summed in bfloat16 or wider, within the bound.
A program may use at most 64 MiB of HBM per device.

```python
import math
import jax
import jax.numpy as jnp
from jax import lax

D = 1024
ROWS = 128
BLK = 8
NODES = 2048
SLOTS = 128
N_PARTS = 16


def set_ends(drawn, key, smallest, high):
    index_at = [jax.random.randint(jax.random.fold_in(key, axis), (), 0, length) for axis, length in enumerate(drawn.shape)]
    main_axis = drawn.shape.index(max(drawn.shape))
    neighbour = index_at[:main_axis] + [(index_at[main_axis] + 1) % drawn.shape[main_axis]] + index_at[main_axis + 1:]
    return drawn.at[tuple(index_at)].set(smallest).at[tuple(neighbour)].set(high)


def levels(rng, dims, split, low, high):
    gain = 1.0
    for dim, blocks in split:
        draws = jax.random.uniform(jax.random.fold_in(jax.random.fold_in(rng, 6), dim), (blocks,), jnp.float32, low / len(split), high / len(split))
        gain = gain * jnp.repeat(jnp.exp(draws), dims[dim] // blocks).reshape((-1,) + (1,) * (len(dims) - 1 - dim))
    return gain


def normal_values(key, shape, deviation, bound, cuts=(), held_as=jnp.bfloat16):
    entries = deviation * jax.random.normal(key, shape, jnp.float32)
    if cuts:
        entries = entries * levels(key, shape, cuts, -0.22, 0.18)
    return jnp.clip(entries, -bound, bound).astype(held_as)


def setup_inputs(seed: int = 0) -> dict:
    splits = jax.random.split(jax.random.key(seed), 11)
    return {
        "feats": normal_values(splits[0], (NODES, D), 1.0, 6.0, ((0, 16), (1, 2))),
        "adj_local": normal_values(splits[1], (NODES, ROWS), ROWS ** -0.5, 0.5, ((0, 16),)),
        "adj_halo": normal_values(splits[2], (NODES, SLOTS), SLOTS ** -0.5, 0.5, ((0, 16),)),
        "w_graph": normal_values(splits[3], (D, D), D ** -0.5, 0.1875, ((1, 2),)),
        "w_query": normal_values(splits[4], (D, D), D ** -0.5, 0.1875, ((1, 2),)),
        "w_key": normal_values(splits[5], (D, D), D ** -0.5, 0.1875, ((1, 2),)),
        "w_value": normal_values(splits[6], (D, D), D ** -0.5, 0.1875, ((1, 2),)),
        "send_rows": set_ends(jax.random.randint(splits[7], (N_PARTS, N_PARTS, BLK), 0, ROWS), jax.random.fold_in(splits[7], 1), 0, ROWS - 1).astype(jnp.int32),
        "send_count": set_ends(jax.random.randint(splits[8], (N_PARTS, N_PARTS), 0, BLK + 1), jax.random.fold_in(splits[8], 1), 0, BLK).astype(jnp.int32),
        "live": set_ends(jax.random.randint(splits[9], (N_PARTS,), ROWS // 2, ROWS + 1), jax.random.fold_in(splits[9], 1), ROWS // 2, ROWS).astype(jnp.int32),
    }


def reference(feats, adj_local, adj_halo, w_graph, w_query, w_key, w_value, send_rows, send_count, live):
    width_all = feats.shape[1]
    feat_blocks = feats.reshape(N_PARTS, ROWS, width_all)
    local_tiles = adj_local.reshape(N_PARTS, ROWS, ROWS)
    halo_tiles = adj_halo.reshape(N_PARTS, ROWS, SLOTS)
    slot_ids = jnp.arange(BLK, dtype=jnp.int32)
    part_ids = jnp.arange(N_PARTS, dtype=jnp.int32)

    def one_part(part_index):
        own_rows = feat_blocks[part_index]
        source_rows = send_rows[:, part_index, :]
        counts = send_count[:, part_index]
        picked = feat_blocks[part_ids[:, None], source_rows]
        picked = jnp.where((slot_ids[None, :] < counts[:, None])[:, :, None], picked, jnp.zeros((), jnp.bfloat16))
        summed = jnp.dot(local_tiles[part_index], own_rows, preferred_element_type=jnp.float32)
        summed = summed + jnp.dot(halo_tiles[part_index], picked.reshape(SLOTS, width_all), preferred_element_type=jnp.float32)
        return summed.astype(jnp.bfloat16)
    convolved = lax.map(one_part, part_ids).reshape(NODES, width_all)
    hidden = jax.nn.gelu(jnp.dot(convolved, w_graph, preferred_element_type=jnp.float32), approximate=False).astype(jnp.bfloat16)
    live_mask = (jnp.arange(ROWS, dtype=jnp.int32)[None, :] < live[:, None]).reshape(NODES, 1)
    queries = jnp.dot(hidden, w_query, preferred_element_type=jnp.float32)
    keys_raw = jnp.dot(hidden, w_key, preferred_element_type=jnp.float32)
    query_feat = jnp.where(live_mask, jax.nn.elu(queries) + 1.0, 0.0).astype(jnp.bfloat16)
    key_feat = jnp.where(live_mask, jax.nn.elu(keys_raw) + 1.0, 0.0).astype(jnp.bfloat16)
    values = jnp.dot(hidden, w_value, preferred_element_type=jnp.float32).astype(jnp.bfloat16)
    query_wide = query_feat.astype(jnp.float32)
    key_wide = key_feat.astype(jnp.float32)
    query_sq = jnp.sum(query_wide * query_wide)
    key_sq = jnp.sum(key_wide * key_wide)
    key_values = lax.dot_general(key_feat, values, (((0,), (0,)), ((), ())), preferred_element_type=jnp.float32)
    key_total = lax.optimization_barrier(jnp.sum(key_wide, axis=0))
    key_summary = key_values / math.sqrt(NODES)
    key_values_b = key_values.astype(jnp.bfloat16)
    numerator = jnp.dot(query_feat, key_values_b, preferred_element_type=jnp.float32)
    denominator = jnp.dot(query_wide, key_total, precision=lax.Precision.HIGHEST)
    inverse = lax.rsqrt(query_sq) * lax.rsqrt(key_sq)
    result = (values.astype(jnp.float32) + numerator * inverse) / (1.0 + denominator * inverse)[:, None]
    return (jnp.where(live_mask, result, 0.0), key_summary)
```

```python
import functools
import math

import jax
import jax.numpy as jnp
from jax import lax
from jax.experimental import pallas as pl
from jax.experimental.pallas import tpu as pltpu
from jax.sharding import PartitionSpec as P

MESH = pl.DeviceIdType.MESH
F32 = jnp.float32
BF16 = jnp.bfloat16


def plain(
    feats, adj_local, adj_halo, w_graph, w_query, w_key, w_value, send_rows, send_count, live
):
    row_count, col_count = feats.shape
    slot_count = send_rows.shape[2]
    picked = feats[send_rows[0]]
    slot_live = jnp.arange(slot_count, dtype=jnp.int32)[None, :] < send_count[0][:, None]
    outgoing = jnp.where(slot_live[:, :, None], picked, jnp.zeros((), jnp.bfloat16))
    incoming = lax.all_to_all(outgoing, "parts", split_axis=0, concat_axis=0, tiled=True)
    halo_rows = incoming.reshape(-1, col_count)
    summed = jnp.dot(adj_local, feats, preferred_element_type=jnp.float32)
    summed = summed + jnp.dot(adj_halo, halo_rows, preferred_element_type=jnp.float32)
    convolved = summed.astype(jnp.bfloat16)
    out_cols = w_graph.shape[1]
    empty = jnp.zeros((row_count, out_cols), jnp.float32)
    weight_rows = w_graph
    projected = jnp.dot(
        lax.all_gather(convolved, "mp", axis=1, tiled=True),
        weight_rows,
        preferred_element_type=jnp.float32,
    )
    hidden = jax.nn.gelu(projected, approximate=False).astype(jnp.bfloat16)
    totals = (empty, empty, empty)
    portion = lax.all_gather(hidden, "mp", axis=1, tiled=True)
    outputs = []
    for running, weight in zip(totals, (w_query, w_key, w_value)):
        weight_rows = weight
        outputs.append(jnp.dot(portion, weight_rows, preferred_element_type=jnp.float32))
    queries, keys_raw, values_wide = tuple(outputs)
    live_mask = jnp.arange(row_count, dtype=jnp.int32)[:, None] < live[0]
    query_feat = jnp.where(live_mask, jax.nn.elu(queries) + 1.0, 0.0).astype(jnp.bfloat16)
    key_feat = jnp.where(live_mask, jax.nn.elu(keys_raw) + 1.0, 0.0).astype(jnp.bfloat16)
    values = values_wide.astype(jnp.bfloat16)
    key_values = lax.dot_general(
        key_feat,
        lax.all_gather(values, "mp", axis=1, tiled=True),
        (((0,), (0,)), ((), ())),
        preferred_element_type=jnp.float32,
    )
    query_wide = query_feat.astype(jnp.float32)
    key_wide = key_feat.astype(jnp.float32)
    key_total = jnp.sum(key_wide, axis=0)
    sq_pair = jnp.stack([jnp.sum(query_wide * query_wide), jnp.sum(key_wide * key_wide)])
    key_values, key_total, sq_pair = lax.psum((key_values, key_total, sq_pair), "parts")
    key_summary = key_values / math.sqrt(lax.axis_size("parts") * row_count)
    numer_part = jnp.dot(
        query_feat, key_values.astype(jnp.bfloat16), preferred_element_type=jnp.float32
    )
    denom_part = jnp.dot(query_wide, key_total, precision=lax.Precision.HIGHEST)
    numerator = lax.psum_scatter(
        numer_part.astype(jnp.bfloat16), "mp", scatter_dimension=1, tiled=True
    ).astype(jnp.float32)
    denominator, sq_pair = lax.psum((denom_part, sq_pair), "mp")
    inverse = lax.rsqrt(sq_pair[0]) * lax.rsqrt(sq_pair[1])
    result = (values.astype(jnp.float32) + numerator * inverse) / (1.0 + denominator * inverse)[
        :, None
    ]
    return (jnp.where(live_mask, result, 0.0), key_summary)


def dot(a, b):
    return jnp.dot(a, b, preferred_element_type=F32)


def kernel(
    n,
    nz,
    feats,
    adj_local,
    adj_halo,
    send_rows,
    send_count,
    live,
    wg,
    wq,
    wk,
    wv,
    out,
    kv_out,
    wbuf,
    outgoing,
    incoming,
    conv,
    hid,
    val,
    query,
    key_t,
    part,
    send1,
    recv1,
    acc2,
    send2,
    recv2,
    send3,
    recv3,
    kvb,
    stat,
    den,
    nsend,
    nrecv,
    wsem,
    osem,
    halo_s,
    halo_r,
    mp_s,
    mp_r,
    s1_s,
    s1_r,
    s2_s,
    s2_r,
    s3_s,
    s3_r,
    gz_s,
    gz_r,
    gy_s,
    gy_r,
    gc_s,
    gc_r,
    st_s,
    st_r,
):
    p = lax.axis_index("parts")
    m = lax.axis_index("mp")
    c, y, z = p % 2, (p // 2) % 2, p // 4
    other = 1 - m
    core_peer = p + 1 - 2 * c
    y_peer = p + 2 - 4 * y
    rows, cols = feats.shape
    slots = outgoing.shape[1]
    half, quarter, piece = cols // 2, cols // 4, cols // n
    sent = []

    def send(src, dst, s_sem, r_sem, device):
        copy = pltpu.make_async_remote_copy(
            src_ref=src,
            dst_ref=dst,
            send_sem=s_sem,
            recv_sem=r_sem,
            device_id=device,
            device_id_type=MESH,
        )
        copy.start()
        sent.append(copy)
        return copy

    loads = []
    for i, w in enumerate((wg, wv, wk, wq)):
        load = pltpu.make_async_copy(w, wbuf.at[i], wsem.at[i])
        load.start()
        loads.append(load)

    barrier = pltpu.get_barrier_semaphore()
    for d in range(1, n):
        pl.semaphore_signal(
            barrier, inc=1, device_id={"parts": lax.rem(p + d, n)}, device_id_type=MESH
        )
    pl.semaphore_signal(barrier, inc=1, device_id={"mp": other}, device_id_type=MESH)

    total = n * slots
    owner = lax.broadcasted_iota(jnp.int32, (total, n), 0) // slots
    is_owner = owner == lax.broadcasted_iota(jnp.int32, (total, n), 1)
    spot = lax.broadcasted_iota(jnp.int32, (total, slots), 0) % slots
    is_spot = spot == lax.broadcasted_iota(jnp.int32, (total, slots), 1)
    spread = jnp.dot(
        is_owner.astype(F32),
        send_rows[...].astype(F32),
        precision=lax.Precision.HIGHEST,
        preferred_element_type=F32,
    )
    index = jnp.sum(jnp.where(is_spot, spread, 0.0), axis=1, keepdims=True)
    count = jnp.sum(
        jnp.where(is_owner, send_count[...].astype(F32), 0.0), axis=1, keepdims=True
    )
    slot_id = jnp.sum(
        jnp.where(is_spot, lax.broadcasted_iota(jnp.int32, (total, slots), 1), 0).astype(F32),
        axis=1,
        keepdims=True,
    )
    index = jnp.where(slot_id < count, index, -1.0)
    node = lax.broadcasted_iota(jnp.int32, (total, rows), 1).astype(F32)
    pick = jnp.where(index == node, 1.0, 0.0).astype(BF16)
    outgoing[...] = dot(pick, feats[...]).reshape(n, slots, cols).astype(BF16)

    pl.semaphore_wait(barrier, n)
    halo = []
    for d in range(1, n):
        to = lax.rem(p + d, n)
        halo.append(
            send(outgoing.at[to], incoming.at[p], halo_s.at[d], halo_r.at[d], {"parts": to})
        )
    incoming[p] = outgoing[p]
    local_sum = dot(adj_local[...], feats[...])
    for copy in halo:
        copy.wait_recv()
    arrived = incoming[...].astype(F32).reshape(total, cols).astype(BF16)
    conv[m] = (local_sum + dot(adj_halo[...], arrived)).astype(BF16)
    swap = send(conv.at[m], conv.at[m], mp_s.at[0], mp_r.at[0], {"mp": other})
    mine = pl.ds(pl.multiple_of(m * cols, cols), cols)
    theirs = pl.ds(pl.multiple_of(other * cols, cols), cols)
    loads[0].wait()
    projected = dot(conv[m], wbuf[0, mine, :])
    swap.wait_recv()
    projected = projected + dot(conv[other], wbuf[0, theirs, :])
    hid[m] = (0.5 * projected * (1.0 + lax.erf(projected * math.sqrt(0.5)))).astype(BF16)
    swap = send(hid.at[m], hid.at[m], mp_s.at[1], mp_r.at[1], {"mp": other})
    for load in loads[1:]:
        load.wait()
    own = hid[m]
    raw_v = dot(own, wbuf[1, mine, :])
    raw_k = dot(own, wbuf[2, mine, :])
    raw_q = dot(own, wbuf[3, mine, :])
    swap.wait_recv()
    rest = hid[other]
    val[m] = (raw_v + dot(rest, wbuf[1, theirs, :])).astype(BF16)
    swap = send(val.at[m], val.at[m], mp_s.at[2], mp_r.at[2], {"mp": other})
    live_mask = lax.broadcasted_iota(jnp.int32, (rows, 1), 0) < live[0]

    def feature(x):
        x = jnp.where(x > 0.0, x + 1.0, jnp.exp(jnp.minimum(x, 0.0)))
        return jnp.where(live_mask, x, 0.0).astype(BF16)

    key_feat = feature(raw_k + dot(rest, wbuf[2, theirs, :]))
    key_wide = key_feat.astype(F32)
    key_t[...] = key_wide.T.astype(BF16)

    keep1 = pl.ds(pl.multiple_of(c * half, half), half)
    give1 = pl.ds(pl.multiple_of((1 - c) * half, half), half)
    keep2 = pl.ds(pl.multiple_of(y * quarter, quarter), quarter)
    give2 = pl.ds(pl.multiple_of((1 - y) * quarter, quarter), quarter)
    step1 = []

    def start1(g, column):
        part[g] = dot(key_t[...], val[column])
        send1[g] = part[g, give1, :].astype(BF16)
        step1.append(
            send(send1.at[g], recv1.at[g], s1_s.at[g], s1_r.at[g], {"parts": core_peer})
        )

    start1(0, m)
    query[...] = feature(raw_q + dot(rest, wbuf[3, theirs, :]))
    query_wide = query[...].astype(F32)
    lane = lax.broadcasted_iota(jnp.int32, (1, 128), 1)
    query_sq = jnp.sum(jnp.sum(query_wide * query_wide, axis=0, keepdims=True), axis=1, keepdims=True)
    key_sq = jnp.sum(jnp.sum(key_wide * key_wide, axis=0, keepdims=True), axis=1, keepdims=True)
    stat[0, :, :cols] = jnp.sum(key_wide, axis=0, keepdims=True)
    stat[0, :, cols:] = jnp.where(lane == 0, query_sq, jnp.where(lane == 1, key_sq, 0.0))
    swap.wait_recv()
    start1(1, other)
    stats = []
    for d in range(1, n):
        stats.append(
            send(stat.at[0], stat.at[d], st_s.at[d], st_r.at[d], {"parts": lax.rem(p + d, n)})
        )
    step2 = []
    for g in range(2):
        step1[g].wait_recv()
        send2[g] = (
            part[g, pl.ds(pl.multiple_of(c * half + (1 - y) * quarter, quarter), quarter), :]
            + recv1[g, give2, :].astype(F32)
        ).astype(BF16)
        step2.append(
            send(send2.at[g], recv2.at[g], s2_s.at[g], s2_r.at[g], {"parts": y_peer})
        )
        acc2[g] = part[
            g, pl.ds(pl.multiple_of(c * half + y * quarter, quarter), quarter), :
        ] + recv1[g, keep2, :].astype(F32)
    step3 = []
    for g in range(2):
        step2[g].wait_recv()
        acc2[g] = acc2[g] + recv2[g].astype(F32)
        send3[g] = acc2[g].astype(BF16)
        for d in range(1, nz):
            to = lax.rem(z + d, nz)
            step3.append(
                send(
                    send3.at[g, pl.ds(pl.multiple_of(to * piece, piece), piece), :],
                    recv3.at[g, d],
                    s3_s.at[g, d],
                    s3_r.at[g, d],
                    {"parts": to * 4 + p % 4},
                )
            )

    def block(zz):
        return pl.ds(pl.multiple_of(c * half + y * quarter + zz * piece, piece), piece)

    gather_z, gather_y, gather_c = [], [], []

    def pass_on(g, column, d):
        place = kvb.at[column, block(lax.rem(z + nz - d, nz)), :]
        gather_y.append(send(place, place, gy_s.at[g, d], gy_r.at[g, d], {"parts": y_peer}))

    for g, column in enumerate((m, other)):
        final = acc2[g, pl.ds(pl.multiple_of(z * piece, piece), piece), :]
        for d in range(1, nz):
            step3[g * (nz - 1) + d - 1].wait_recv()
            final = final + recv3[g, d].astype(F32)
        kvb[column, block(z), :] = final.astype(BF16)
        place = kvb.at[column, block(z), :]
        for d in range(1, nz):
            gather_z.append(
                send(
                    place,
                    place,
                    gz_s.at[g, d],
                    gz_r.at[g, d],
                    {"parts": lax.rem(z + d, nz) * 4 + p % 4},
                )
            )
        pass_on(g, column, 0)

    for copy in stats:
        copy.wait_recv()
    sums = stat[0]
    for d in range(1, n):
        sums = sums + stat[d]
    den[m, :rows, :] = jnp.broadcast_to(
        jnp.sum(query_wide * sums[:, :cols], axis=1, keepdims=True), (rows, 128)
    )
    den[m, rows:, :] = jnp.broadcast_to(sums[:, cols:], (8, 128))
    den_swap = send(den.at[m], den.at[m], mp_s.at[3], mp_r.at[3], {"mp": other})

    def keep_block(column, yy):
        return kvb.at[
            column, pl.ds(pl.multiple_of(c * half + yy * quarter, quarter), quarter), :
        ]

    for g, column in enumerate((m, other)):
        for d in range(1, nz):
            gather_z[g * (nz - 1) + d - 1].wait_recv()
            pass_on(g, column, d)
        place = keep_block(column, y)
        gather_c.append(send(place, place, gc_s.at[g, 0], gc_r.at[g, 0], {"parts": core_peer}))
    for g, column in enumerate((m, other)):
        gather_y[g].wait_recv()
        for d in range(1, nz):
            gather_y[2 + g * (nz - 1) + d - 1].wait_recv()
        place = keep_block(column, 1 - y)
        gather_c.append(send(place, place, gc_s.at[g, 1], gc_r.at[g, 1], {"parts": core_peer}))
    gather_c[0].wait_recv()
    gather_c[2].wait_recv()
    numerator = dot(query[...], kvb[m])
    gather_c[1].wait_recv()
    gather_c[3].wait_recv()
    nsend[...] = dot(query[...], kvb[other]).astype(BF16)
    swap = send(nsend, nrecv, mp_s.at[4], mp_r.at[4], {"mp": other})
    stores = []
    for g in range(2):
        store = pltpu.make_async_copy(kvb.at[g], kv_out.at[:, pl.ds(g * cols, cols)], osem.at[g])
        store.start()
        stores.append(store)
    den_swap.wait_recv()
    square = den[0, rows : rows + 1, :] + den[1, rows : rows + 1, :]
    query_sq = jnp.sum(jnp.where(lane == 0, square, 0.0), axis=1, keepdims=True)
    key_sq = jnp.sum(jnp.where(lane == 1, square, 0.0), axis=1, keepdims=True)
    inverse = lax.rsqrt(query_sq) * lax.rsqrt(key_sq)
    denominator = den[0, :rows, 0:1] + den[1, :rows, 0:1]
    scale = 1.0 + denominator * inverse
    swap.wait_recv()
    numerator = numerator + nrecv[...].astype(F32)
    result = (val[m].astype(F32) + numerator * inverse) / scale
    out[...] = jnp.where(live_mask, result, 0.0)
    for store in stores:
        store.wait()
    for copy in sent:
        copy.wait_send()


def fused(
    feats, adj_local, adj_halo, w_graph, w_query, w_key, w_value, send_rows, send_count, live
):
    n = lax.axis_size("parts")
    nz = n // 4
    rows, cols = feats.shape
    slots = send_rows.shape[2]
    depth = w_graph.shape[0]
    half, quarter, piece = cols // 2, cols // 4, cols // n
    vmem = pl.BlockSpec(memory_space=pltpu.VMEM)
    hbm = pl.BlockSpec(memory_space=pl.ANY)
    dma = pltpu.SemaphoreType.DMA
    out, kv = pl.pallas_call(
        functools.partial(kernel, n, nz),
        out_shape=(
            jax.ShapeDtypeStruct((rows, cols), F32),
            jax.ShapeDtypeStruct((cols, depth), BF16),
        ),
        in_specs=[vmem] * 5 + [pl.BlockSpec(memory_space=pltpu.SMEM)] + [hbm] * 4,
        out_specs=(vmem, hbm),
        scratch_shapes=[
            pltpu.VMEM((4, depth, cols), BF16),
            pltpu.VMEM((n, slots, cols), BF16),
            pltpu.VMEM((n, slots, cols), BF16),
            pltpu.VMEM((2, rows, cols), BF16),
            pltpu.VMEM((2, rows, cols), BF16),
            pltpu.VMEM((2, rows, cols), BF16),
            pltpu.VMEM((rows, cols), BF16),
            pltpu.VMEM((cols, rows), BF16),
            pltpu.VMEM((2, cols, cols), F32),
            pltpu.VMEM((2, half, cols), BF16),
            pltpu.VMEM((2, half, cols), BF16),
            pltpu.VMEM((2, quarter, cols), F32),
            pltpu.VMEM((2, quarter, cols), BF16),
            pltpu.VMEM((2, quarter, cols), BF16),
            pltpu.VMEM((2, quarter, cols), BF16),
            pltpu.VMEM((2, nz, piece, cols), BF16),
            pltpu.VMEM((2, cols, cols), BF16),
            pltpu.VMEM((n, 1, cols + 128), F32),
            pltpu.VMEM((2, rows + 8, 128), F32),
            pltpu.VMEM((rows, cols), BF16),
            pltpu.VMEM((rows, cols), BF16),
            dma((4,)),
            dma((2,)),
            dma((n,)),
            dma((n,)),
            dma((5,)),
            dma((5,)),
            dma((2,)),
            dma((2,)),
            dma((2,)),
            dma((2,)),
            dma((2, nz)),
            dma((2, nz)),
            dma((2, nz)),
            dma((2, nz)),
            dma((2, nz)),
            dma((2, nz)),
            dma((2, 2)),
            dma((2, 2)),
            dma((n,)),
            dma((n,)),
        ],
        compiler_params=pltpu.CompilerParams(collective_id=0, has_side_effects=True),
    )(
        feats,
        adj_local,
        adj_halo,
        send_rows[0],
        send_count,
        live,
        w_graph,
        w_query,
        w_key,
        w_value,
    )
    return out, kv.astype(F32) / math.sqrt(n * rows)


def local(*args):
    n = lax.axis_size("parts")
    rows, cols = args[0].shape
    slots = args[7].shape[2]
    fits = (
        lax.axis_size("mp") == 2
        and n % 4 == 0
        and cols % (16 * n) == 0
        and rows % 16 == 0
        and (n * slots) % 16 == 0
        and slots % 8 == 0
    )
    return fused(*args) if fits else plain(*args)


def solution(mesh):
    return jax.shard_map(
        local,
        mesh=mesh,
        in_specs=(
            P("parts", "mp"),
            P("parts", None),
            P("parts", None),
            P(None, "mp"),
            P(None, "mp"),
            P(None, "mp"),
            P(None, "mp"),
            P("parts", None, None),
            P("parts", None),
            P("parts"),
        ),
        out_specs=(P("parts", "mp"), P("mp", None)),
        check_vma=False,
    )
```

```python
import functools
import math

import jax
import jax.numpy as jnp
from jax import lax
from jax.experimental import pallas as pl
from jax.experimental.pallas import tpu as pltpu
from jax.sharding import PartitionSpec as P

MESH = pl.DeviceIdType.MESH
F32 = jnp.float32
BF16 = jnp.bfloat16


def plain(
    feats, adj_local, adj_halo, w_graph, w_query, w_key, w_value, send_rows, send_count, live
):
    row_count, col_count = feats.shape
    slot_count = send_rows.shape[2]
    picked = feats[send_rows[0]]
    slot_live = jnp.arange(slot_count, dtype=jnp.int32)[None, :] < send_count[0][:, None]
    outgoing = jnp.where(slot_live[:, :, None], picked, jnp.zeros((), jnp.bfloat16))
    incoming = lax.all_to_all(outgoing, "parts", split_axis=0, concat_axis=0, tiled=True)
    halo_rows = incoming.reshape(-1, col_count)
    summed = jnp.dot(adj_local, feats, preferred_element_type=jnp.float32)
    summed = summed + jnp.dot(adj_halo, halo_rows, preferred_element_type=jnp.float32)
    convolved = summed.astype(jnp.bfloat16)
    out_cols = w_graph.shape[1]
    empty = jnp.zeros((row_count, out_cols), jnp.float32)
    weight_rows = w_graph
    projected = jnp.dot(
        lax.all_gather(convolved, "mp", axis=1, tiled=True),
        weight_rows,
        preferred_element_type=jnp.float32,
    )
    hidden = jax.nn.gelu(projected, approximate=False).astype(jnp.bfloat16)
    totals = (empty, empty, empty)
    portion = lax.all_gather(hidden, "mp", axis=1, tiled=True)
    outputs = []
    for running, weight in zip(totals, (w_query, w_key, w_value)):
        weight_rows = weight
        outputs.append(jnp.dot(portion, weight_rows, preferred_element_type=jnp.float32))
    queries, keys_raw, values_wide = tuple(outputs)
    live_mask = jnp.arange(row_count, dtype=jnp.int32)[:, None] < live[0]
    query_feat = jnp.where(live_mask, jax.nn.elu(queries) + 1.0, 0.0).astype(jnp.bfloat16)
    key_feat = jnp.where(live_mask, jax.nn.elu(keys_raw) + 1.0, 0.0).astype(jnp.bfloat16)
    values = values_wide.astype(jnp.bfloat16)
    key_values = lax.dot_general(
        key_feat,
        lax.all_gather(values, "mp", axis=1, tiled=True),
        (((0,), (0,)), ((), ())),
        preferred_element_type=jnp.float32,
    )
    query_wide = query_feat.astype(jnp.float32)
    key_wide = key_feat.astype(jnp.float32)
    key_total = jnp.sum(key_wide, axis=0)
    sq_pair = jnp.stack([jnp.sum(query_wide * query_wide), jnp.sum(key_wide * key_wide)])
    key_values, key_total, sq_pair = lax.psum((key_values, key_total, sq_pair), "parts")
    key_summary = key_values / math.sqrt(lax.axis_size("parts") * row_count)
    numer_part = jnp.dot(
        query_feat, key_values.astype(jnp.bfloat16), preferred_element_type=jnp.float32
    )
    denom_part = jnp.dot(query_wide, key_total, precision=lax.Precision.HIGHEST)
    numerator = lax.psum_scatter(
        numer_part.astype(jnp.bfloat16), "mp", scatter_dimension=1, tiled=True
    ).astype(jnp.float32)
    denominator, sq_pair = lax.psum((denom_part, sq_pair), "mp")
    inverse = lax.rsqrt(sq_pair[0]) * lax.rsqrt(sq_pair[1])
    result = (values.astype(jnp.float32) + numerator * inverse) / (1.0 + denominator * inverse)[
        :, None
    ]
    return (jnp.where(live_mask, result, 0.0), key_summary)


def dot(a, b):
    return jnp.dot(a, b, preferred_element_type=F32)


def kernel(
    n,
    nz,
    feats_in,
    adj_local_in,
    adj_halo_in,
    send_rows_in,
    send_count_in,
    live,
    wg,
    wq,
    wk,
    wv,
    out,
    kv_out,
    feats,
    adj_local,
    adj_halo,
    send_rows,
    send_count,
    wbuf,
    outgoing,
    incoming,
    conv,
    hid,
    val,
    query,
    key_t,
    part,
    send1,
    recv1,
    acc2,
    send2,
    recv2,
    send3,
    recv3,
    kvb,
    stat,
    den,
    nsend,
    nrecv,
    isem,
    wsem,
    osem,
    halo_s,
    halo_r,
    mp_s,
    mp_r,
    s1_s,
    s1_r,
    s2_s,
    s2_r,
    s3_s,
    s3_r,
    gz_s,
    gz_r,
    gy_s,
    gy_r,
    gc_s,
    gc_r,
    st_s,
    st_r,
):
    p = lax.axis_index("parts")
    m = lax.axis_index("mp")
    c, y, z = p % 2, (p // 2) % 2, p // 4
    other = 1 - m
    core_peer = p + 1 - 2 * c
    y_peer = p + 2 - 4 * y
    rows, cols = feats.shape
    slots = outgoing.shape[1]
    half, quarter, piece = cols // 2, cols // 4, cols // n
    sent = []

    def send(src, dst, s_sem, r_sem, device):
        copy = pltpu.make_async_remote_copy(
            src_ref=src,
            dst_ref=dst,
            send_sem=s_sem,
            recv_sem=r_sem,
            device_id=device,
            device_id_type=MESH,
        )
        copy.start()
        sent.append(copy)
        return copy

    inputs = []
    for i, (source, place) in enumerate(
        (
            (send_rows_in, send_rows),
            (send_count_in, send_count),
            (feats_in, feats),
            (adj_local_in, adj_local),
            (adj_halo_in, adj_halo),
        )
    ):
        load = pltpu.make_async_copy(source, place, isem.at[i])
        load.start()
        inputs.append(load)
    loads = []
    for i, w in enumerate((wg, wv, wk, wq)):
        load = pltpu.make_async_copy(w, wbuf.at[i], wsem.at[i])
        load.start()
        loads.append(load)

    barrier = pltpu.get_barrier_semaphore()
    for d in range(1, n):
        pl.semaphore_signal(
            barrier, inc=1, device_id={"parts": lax.rem(p + d, n)}, device_id_type=MESH
        )
    pl.semaphore_signal(barrier, inc=1, device_id={"mp": other}, device_id_type=MESH)

    for load in inputs:
        load.wait()

    total = n * slots
    owner = lax.broadcasted_iota(jnp.int32, (total, n), 0) // slots
    is_owner = owner == lax.broadcasted_iota(jnp.int32, (total, n), 1)
    spot = lax.broadcasted_iota(jnp.int32, (total, slots), 0) % slots
    is_spot = spot == lax.broadcasted_iota(jnp.int32, (total, slots), 1)
    spread = lax.dot_general(
        is_owner.astype(F32),
        send_rows[...].astype(F32),
        (((1,), (1,)), ((), ())),
        precision=lax.Precision.HIGHEST,
        preferred_element_type=F32,
    )
    index = jnp.sum(jnp.where(is_spot, spread, 0.0), axis=1, keepdims=True)
    count = jnp.sum(
        jnp.where(is_owner, send_count[...].astype(F32), 0.0), axis=1, keepdims=True
    )
    slot_id = jnp.sum(
        jnp.where(is_spot, lax.broadcasted_iota(jnp.int32, (total, slots), 1), 0).astype(F32),
        axis=1,
        keepdims=True,
    )
    index = jnp.where(slot_id < count, index, -1.0)
    node = lax.broadcasted_iota(jnp.int32, (total, rows), 1).astype(F32)
    pick = jnp.where(index == node, 1.0, 0.0).astype(BF16)
    outgoing[...] = dot(pick, feats[...]).reshape(n, slots, cols).astype(BF16)

    pl.semaphore_wait(barrier, n)
    halo = []
    for d in range(1, n):
        to = lax.rem(p + d, n)
        halo.append(
            send(outgoing.at[to], incoming.at[p], halo_s.at[d], halo_r.at[d], {"parts": to})
        )
    incoming[p] = outgoing[p]
    local_sum = dot(adj_local[...], feats[...])
    for copy in halo:
        copy.wait_recv()
    arrived = incoming[...].astype(F32).reshape(total, cols).astype(BF16)
    conv[m] = (local_sum + dot(adj_halo[...], arrived)).astype(BF16)
    swap = send(conv.at[m], conv.at[m], mp_s.at[0], mp_r.at[0], {"mp": other})
    mine = pl.ds(pl.multiple_of(m * cols, cols), cols)
    theirs = pl.ds(pl.multiple_of(other * cols, cols), cols)
    loads[0].wait()
    projected = dot(conv[m], wbuf[0, mine, :])
    swap.wait_recv()
    projected = projected + dot(conv[other], wbuf[0, theirs, :])
    hid[m] = (0.5 * projected * (1.0 + lax.erf(projected * math.sqrt(0.5)))).astype(BF16)
    swap = send(hid.at[m], hid.at[m], mp_s.at[1], mp_r.at[1], {"mp": other})
    for load in loads[1:]:
        load.wait()
    own = hid[m]
    raw_v = dot(own, wbuf[1, mine, :])
    raw_k = dot(own, wbuf[2, mine, :])
    raw_q = dot(own, wbuf[3, mine, :])
    swap.wait_recv()
    rest = hid[other]
    val[m] = (raw_v + dot(rest, wbuf[1, theirs, :])).astype(BF16)
    swap = send(val.at[m], val.at[m], mp_s.at[2], mp_r.at[2], {"mp": other})
    live_mask = lax.broadcasted_iota(jnp.int32, (rows, 1), 0) < live[0]

    def feature(x):
        x = jnp.where(x > 0.0, x + 1.0, jnp.exp(jnp.minimum(x, 0.0)))
        return jnp.where(live_mask, x, 0.0).astype(BF16)

    key_feat = feature(raw_k + dot(rest, wbuf[2, theirs, :]))
    key_wide = key_feat.astype(F32)
    key_t[...] = key_wide.T.astype(BF16)

    keep1 = pl.ds(pl.multiple_of(c * half, half), half)
    give1 = pl.ds(pl.multiple_of((1 - c) * half, half), half)
    keep2 = pl.ds(pl.multiple_of(y * quarter, quarter), quarter)
    give2 = pl.ds(pl.multiple_of((1 - y) * quarter, quarter), quarter)
    step1 = []

    def start1(g, column):
        send1[g] = dot(key_t[give1, :], val[column]).astype(BF16)
        step1.append(
            send(send1.at[g], recv1.at[g], s1_s.at[g], s1_r.at[g], {"parts": core_peer})
        )
        part[g] = dot(key_t[keep1, :], val[column])

    start1(0, m)
    query[...] = feature(raw_q + dot(rest, wbuf[3, theirs, :]))
    query_wide = query[...].astype(F32)
    lane = lax.broadcasted_iota(jnp.int32, (1, 128), 1)
    query_sq = jnp.sum(jnp.sum(query_wide * query_wide, axis=0, keepdims=True), axis=1, keepdims=True)
    key_sq = jnp.sum(jnp.sum(key_wide * key_wide, axis=0, keepdims=True), axis=1, keepdims=True)
    stat[0, :, :cols] = jnp.sum(key_wide, axis=0, keepdims=True)
    stat[0, :, cols:] = jnp.where(lane == 0, query_sq, jnp.where(lane == 1, key_sq, 0.0))
    swap.wait_recv()
    start1(1, other)
    stats = []
    for d in range(1, n):
        stats.append(
            send(stat.at[0], stat.at[d], st_s.at[d], st_r.at[d], {"parts": lax.rem(p + d, n)})
        )
    step2 = []
    for g in range(2):
        step1[g].wait_recv()
        send2[g] = (
            part[g, give2, :]
            + recv1[g, give2, :].astype(F32)
        ).astype(BF16)
        step2.append(
            send(send2.at[g], recv2.at[g], s2_s.at[g], s2_r.at[g], {"parts": y_peer})
        )
        acc2[g] = part[g, keep2, :] + recv1[g, keep2, :].astype(F32)
    step3 = []
    for g in range(2):
        step2[g].wait_recv()
        acc2[g] = acc2[g] + recv2[g].astype(F32)
        send3[g] = acc2[g].astype(BF16)
        for d in range(1, nz):
            to = lax.rem(z + d, nz)
            step3.append(
                send(
                    send3.at[g, pl.ds(pl.multiple_of(to * piece, piece), piece), :],
                    recv3.at[g, d],
                    s3_s.at[g, d],
                    s3_r.at[g, d],
                    {"parts": to * 4 + p % 4},
                )
            )

    def block(zz):
        return pl.ds(pl.multiple_of(c * half + y * quarter + zz * piece, piece), piece)

    gather_z, gather_y, gather_c = [], [], []

    def pass_on(g, column, d):
        place = kvb.at[column, block(lax.rem(z + nz - d, nz)), :]
        gather_y.append(send(place, place, gy_s.at[g, d], gy_r.at[g, d], {"parts": y_peer}))

    for g, column in enumerate((m, other)):
        final = acc2[g, pl.ds(pl.multiple_of(z * piece, piece), piece), :]
        for d in range(1, nz):
            step3[g * (nz - 1) + d - 1].wait_recv()
            final = final + recv3[g, d].astype(F32)
        kvb[column, block(z), :] = final.astype(BF16)
        place = kvb.at[column, block(z), :]
        for d in range(1, nz):
            gather_z.append(
                send(
                    place,
                    place,
                    gz_s.at[g, d],
                    gz_r.at[g, d],
                    {"parts": lax.rem(z + d, nz) * 4 + p % 4},
                )
            )
        pass_on(g, column, 0)

    for copy in stats:
        copy.wait_recv()
    sums = stat[0]
    for d in range(1, n):
        sums = sums + stat[d]
    den[m, :rows, :] = jnp.broadcast_to(
        jnp.sum(query_wide * sums[:, :cols], axis=1, keepdims=True), (rows, 128)
    )
    den[m, rows:, :] = jnp.broadcast_to(sums[:, cols:], (8, 128))
    den_swap = send(den.at[m], den.at[m], mp_s.at[3], mp_r.at[3], {"mp": other})

    def keep_block(column, yy):
        return kvb.at[
            column, pl.ds(pl.multiple_of(c * half + yy * quarter, quarter), quarter), :
        ]

    for g, column in enumerate((m, other)):
        for d in range(1, nz):
            gather_z[g * (nz - 1) + d - 1].wait_recv()
            pass_on(g, column, d)
        place = keep_block(column, y)
        gather_c.append(send(place, place, gc_s.at[g, 0], gc_r.at[g, 0], {"parts": core_peer}))
    for g, column in enumerate((m, other)):
        gather_y[g].wait_recv()
        for d in range(1, nz):
            gather_y[2 + g * (nz - 1) + d - 1].wait_recv()
        place = keep_block(column, 1 - y)
        gather_c.append(send(place, place, gc_s.at[g, 1], gc_r.at[g, 1], {"parts": core_peer}))
    gather_c[0].wait_recv()
    gather_c[2].wait_recv()
    numerator = dot(query[...], kvb[m])
    gather_c[1].wait_recv()
    gather_c[3].wait_recv()
    nsend[...] = dot(query[...], kvb[other]).astype(BF16)
    swap = send(nsend, nrecv, mp_s.at[4], mp_r.at[4], {"mp": other})
    stores = []
    for g in range(2):
        store = pltpu.make_async_copy(kvb.at[g], kv_out.at[:, pl.ds(g * cols, cols)], osem.at[g])
        store.start()
        stores.append(store)
    den_swap.wait_recv()
    square = den[0, rows : rows + 1, :] + den[1, rows : rows + 1, :]
    query_sq = jnp.sum(jnp.where(lane == 0, square, 0.0), axis=1, keepdims=True)
    key_sq = jnp.sum(jnp.where(lane == 1, square, 0.0), axis=1, keepdims=True)
    inverse = lax.rsqrt(query_sq) * lax.rsqrt(key_sq)
    denominator = den[0, :rows, 0:1] + den[1, :rows, 0:1]
    scale = 1.0 + denominator * inverse
    swap.wait_recv()
    numerator = numerator + nrecv[...].astype(F32)
    result = (val[m].astype(F32) + numerator * inverse) / scale
    out[...] = jnp.where(live_mask, result, 0.0)
    for store in stores:
        store.wait()
    for copy in sent:
        copy.wait_send()


def fused(
    feats, adj_local, adj_halo, w_graph, w_query, w_key, w_value, send_rows, send_count, live
):
    n = lax.axis_size("parts")
    nz = n // 4
    rows, cols = feats.shape
    slots = send_rows.shape[2]
    depth = w_graph.shape[0]
    half, quarter, piece = cols // 2, cols // 4, cols // n
    vmem = pl.BlockSpec(memory_space=pltpu.VMEM)
    hbm = pl.BlockSpec(memory_space=pltpu.HBM)
    dma = pltpu.SemaphoreType.DMA
    place = functools.partial(pltpu.with_memory_space_constraint, memory_space=pltpu.HBM)
    out, kv = pl.pallas_call(
        functools.partial(kernel, n, nz),
        out_shape=(
            jax.ShapeDtypeStruct((rows, cols), F32),
            jax.ShapeDtypeStruct((cols, depth), BF16),
        ),
        in_specs=[hbm] * 5 + [pl.BlockSpec(memory_space=pltpu.SMEM)] + [hbm] * 4,
        out_specs=(vmem, pl.BlockSpec(memory_space=pl.ANY)),
        scratch_shapes=[
            pltpu.VMEM(feats.shape, BF16),
            pltpu.VMEM(adj_local.shape, BF16),
            pltpu.VMEM(adj_halo.shape, BF16),
            pltpu.VMEM((slots, n), jnp.int32),
            pltpu.VMEM((1, n), jnp.int32),
            pltpu.VMEM((4, depth, cols), BF16),
            pltpu.VMEM((n, slots, cols), BF16),
            pltpu.VMEM((n, slots, cols), BF16),
            pltpu.VMEM((2, rows, cols), BF16),
            pltpu.VMEM((2, rows, cols), BF16),
            pltpu.VMEM((2, rows, cols), BF16),
            pltpu.VMEM((rows, cols), BF16),
            pltpu.VMEM((cols, rows), BF16),
            pltpu.VMEM((2, half, cols), F32),
            pltpu.VMEM((2, half, cols), BF16),
            pltpu.VMEM((2, half, cols), BF16),
            pltpu.VMEM((2, quarter, cols), F32),
            pltpu.VMEM((2, quarter, cols), BF16),
            pltpu.VMEM((2, quarter, cols), BF16),
            pltpu.VMEM((2, quarter, cols), BF16),
            pltpu.VMEM((2, nz, piece, cols), BF16),
            pltpu.VMEM((2, cols, cols), BF16),
            pltpu.VMEM((n, 1, cols + 128), F32),
            pltpu.VMEM((2, rows + 8, 128), F32),
            pltpu.VMEM((rows, cols), BF16),
            pltpu.VMEM((rows, cols), BF16),
            dma((5,)),
            dma((4,)),
            dma((2,)),
            dma((n,)),
            dma((n,)),
            dma((5,)),
            dma((5,)),
            dma((2,)),
            dma((2,)),
            dma((2,)),
            dma((2,)),
            dma((2, nz)),
            dma((2, nz)),
            dma((2, nz)),
            dma((2, nz)),
            dma((2, nz)),
            dma((2, nz)),
            dma((2, 2)),
            dma((2, 2)),
            dma((n,)),
            dma((n,)),
        ],
        compiler_params=pltpu.CompilerParams(
            collective_id=0, has_side_effects=True, vmem_limit_bytes=24 * 1024 * 1024
        ),
    )(
        *(place(a) for a in (feats, adj_local, adj_halo, send_rows[0].T, send_count)),
        live,
        *(place(w) for w in (w_graph, w_query, w_key, w_value)),
    )
    return out, kv.astype(F32) / math.sqrt(n * rows)


def local(*args):
    n = lax.axis_size("parts")
    rows, cols = args[0].shape
    slots = args[7].shape[2]
    fits = (
        lax.axis_size("mp") == 2
        and n % 4 == 0
        and cols % (16 * n) == 0
        and rows % 16 == 0
        and (n * slots) % 16 == 0
        and slots % 8 == 0
    )
    return fused(*args) if fits else plain(*args)


def solution(mesh):
    return jax.shard_map(
        local,
        mesh=mesh,
        in_specs=(
            P("parts", "mp"),
            P("parts", None),
            P("parts", None),
            P(None, "mp"),
            P(None, "mp"),
            P(None, "mp"),
            P(None, "mp"),
            P("parts", None, None),
            P("parts", None),
            P("parts"),
        ),
        out_specs=(P("parts", "mp"), P("mp", None)),
        check_vma=False,
    )
```

```python
import functools
import math

import jax
import jax.numpy as jnp
from jax import lax
from jax.experimental import pallas as pl
from jax.experimental.pallas import tpu as pltpu
from jax.sharding import PartitionSpec as P

MESH = pl.DeviceIdType.MESH
F32 = jnp.float32
BF16 = jnp.bfloat16


def plain(
    feats, adj_local, adj_halo, w_graph, w_query, w_key, w_value, send_rows, send_count, live
):
    row_count, col_count = feats.shape
    slot_count = send_rows.shape[2]
    picked = feats[send_rows[0]]
    slot_live = jnp.arange(slot_count, dtype=jnp.int32)[None, :] < send_count[0][:, None]
    outgoing = jnp.where(slot_live[:, :, None], picked, jnp.zeros((), jnp.bfloat16))
    incoming = lax.all_to_all(outgoing, "parts", split_axis=0, concat_axis=0, tiled=True)
    halo_rows = incoming.reshape(-1, col_count)
    summed = jnp.dot(adj_local, feats, preferred_element_type=jnp.float32)
    summed = summed + jnp.dot(adj_halo, halo_rows, preferred_element_type=jnp.float32)
    convolved = summed.astype(jnp.bfloat16)
    out_cols = w_graph.shape[1]
    empty = jnp.zeros((row_count, out_cols), jnp.float32)
    weight_rows = w_graph
    projected = jnp.dot(
        lax.all_gather(convolved, "mp", axis=1, tiled=True),
        weight_rows,
        preferred_element_type=jnp.float32,
    )
    hidden = jax.nn.gelu(projected, approximate=False).astype(jnp.bfloat16)
    totals = (empty, empty, empty)
    portion = lax.all_gather(hidden, "mp", axis=1, tiled=True)
    outputs = []
    for running, weight in zip(totals, (w_query, w_key, w_value)):
        weight_rows = weight
        outputs.append(jnp.dot(portion, weight_rows, preferred_element_type=jnp.float32))
    queries, keys_raw, values_wide = tuple(outputs)
    live_mask = jnp.arange(row_count, dtype=jnp.int32)[:, None] < live[0]
    query_feat = jnp.where(live_mask, jax.nn.elu(queries) + 1.0, 0.0).astype(jnp.bfloat16)
    key_feat = jnp.where(live_mask, jax.nn.elu(keys_raw) + 1.0, 0.0).astype(jnp.bfloat16)
    values = values_wide.astype(jnp.bfloat16)
    key_values = lax.dot_general(
        key_feat,
        lax.all_gather(values, "mp", axis=1, tiled=True),
        (((0,), (0,)), ((), ())),
        preferred_element_type=jnp.float32,
    )
    query_wide = query_feat.astype(jnp.float32)
    key_wide = key_feat.astype(jnp.float32)
    key_total = jnp.sum(key_wide, axis=0)
    sq_pair = jnp.stack([jnp.sum(query_wide * query_wide), jnp.sum(key_wide * key_wide)])
    key_values, key_total, sq_pair = lax.psum((key_values, key_total, sq_pair), "parts")
    key_summary = key_values / math.sqrt(lax.axis_size("parts") * row_count)
    numer_part = jnp.dot(
        query_feat, key_values.astype(jnp.bfloat16), preferred_element_type=jnp.float32
    )
    denom_part = jnp.dot(query_wide, key_total, precision=lax.Precision.HIGHEST)
    numerator = lax.psum_scatter(
        numer_part.astype(jnp.bfloat16), "mp", scatter_dimension=1, tiled=True
    ).astype(jnp.float32)
    denominator, sq_pair = lax.psum((denom_part, sq_pair), "mp")
    inverse = lax.rsqrt(sq_pair[0]) * lax.rsqrt(sq_pair[1])
    result = (values.astype(jnp.float32) + numerator * inverse) / (1.0 + denominator * inverse)[
        :, None
    ]
    return (jnp.where(live_mask, result, 0.0), key_summary)


def dot(a, b):
    return jnp.dot(a, b, preferred_element_type=F32)


def kernel(
    n,
    nz,
    feats_in,
    adj_local_in,
    adj_halo_in,
    send_rows_in,
    send_count_in,
    live,
    wg,
    wq,
    wk,
    wv,
    out,
    kv_out,
    feats,
    adj_local,
    adj_halo,
    send_rows,
    send_count,
    wbuf,
    outgoing,
    incoming,
    conv,
    hid,
    val,
    query,
    key_t,
    part,
    send1,
    recv1,
    acc2,
    send2,
    recv2,
    send3,
    recv3,
    kvb,
    stat,
    den,
    nsend,
    nrecv,
    isem,
    wsem,
    osem,
    halo_s,
    halo_r,
    mp_s,
    mp_r,
    s1_s,
    s1_r,
    s2_s,
    s2_r,
    s3_s,
    s3_r,
    gz_s,
    gz_r,
    gy_s,
    gy_r,
    gc_s,
    gc_r,
    st_s,
    st_r,
):
    p = lax.axis_index("parts")
    m = lax.axis_index("mp")
    c, y, z = p % 2, (p // 2) % 2, p // 4
    other = 1 - m
    core_peer = p + 1 - 2 * c
    y_peer = p + 2 - 4 * y
    rows, cols = feats.shape
    slots = outgoing.shape[1]
    half, quarter, piece = cols // 2, cols // 4, cols // n
    sent = []

    def send(src, dst, s_sem, r_sem, device):
        copy = pltpu.make_async_remote_copy(
            src_ref=src,
            dst_ref=dst,
            send_sem=s_sem,
            recv_sem=r_sem,
            device_id=device,
            device_id_type=MESH,
        )
        copy.start()
        sent.append(copy)
        return copy

    inputs = []
    for i, (source, place) in enumerate(
        (
            (send_rows_in, send_rows),
            (send_count_in, send_count),
            (feats_in, feats),
            (adj_local_in, adj_local),
            (adj_halo_in, adj_halo),
        )
    ):
        load = pltpu.make_async_copy(source, place, isem.at[i])
        load.start()
        inputs.append(load)
    loads = []
    for i, w in enumerate((wg, wv, wk, wq)):
        load = pltpu.make_async_copy(w, wbuf.at[i], wsem.at[i])
        load.start()
        loads.append(load)

    barrier = pltpu.get_barrier_semaphore()
    for d in range(1, n):
        pl.semaphore_signal(
            barrier, inc=1, device_id={"parts": lax.rem(p + d, n)}, device_id_type=MESH
        )
    pl.semaphore_signal(barrier, inc=1, device_id={"mp": other}, device_id_type=MESH)

    for load in inputs:
        load.wait()

    total = n * slots
    owner = lax.broadcasted_iota(jnp.int32, (total, n), 0) // slots
    is_owner = owner == lax.broadcasted_iota(jnp.int32, (total, n), 1)
    spot = lax.broadcasted_iota(jnp.int32, (total, slots), 0) % slots
    is_spot = spot == lax.broadcasted_iota(jnp.int32, (total, slots), 1)
    spread = lax.dot_general(
        is_owner.astype(F32),
        send_rows[...].astype(F32),
        (((1,), (1,)), ((), ())),
        precision=lax.Precision.HIGHEST,
        preferred_element_type=F32,
    )
    index = jnp.sum(jnp.where(is_spot, spread, 0.0), axis=1, keepdims=True)
    count = jnp.sum(
        jnp.where(is_owner, send_count[...].astype(F32), 0.0), axis=1, keepdims=True
    )
    slot_id = jnp.sum(
        jnp.where(is_spot, lax.broadcasted_iota(jnp.int32, (total, slots), 1), 0).astype(F32),
        axis=1,
        keepdims=True,
    )
    index = jnp.where(slot_id < count, index, -1.0)
    node = lax.broadcasted_iota(jnp.int32, (total, rows), 1).astype(F32)
    pick = jnp.where(index == node, 1.0, 0.0).astype(BF16)
    outgoing[...] = dot(pick, feats[...]).reshape(n, slots, cols).astype(BF16)

    pl.semaphore_wait(barrier, n)
    halo = []
    for d in range(1, n):
        to = lax.rem(p + d, n)
        halo.append(
            send(outgoing.at[to], incoming.at[p], halo_s.at[d], halo_r.at[d], {"parts": to})
        )
    incoming[p] = outgoing[p]
    local_sum = dot(adj_local[...], feats[...])
    for copy in halo:
        copy.wait_recv()
    arrived = incoming[...].astype(F32).reshape(total, cols).astype(BF16)
    conv[m] = (local_sum + dot(adj_halo[...], arrived)).astype(BF16)
    swap = send(conv.at[m], conv.at[m], mp_s.at[0], mp_r.at[0], {"mp": other})
    mine = pl.ds(pl.multiple_of(m * cols, cols), cols)
    theirs = pl.ds(pl.multiple_of(other * cols, cols), cols)
    loads[0].wait()
    projected = dot(conv[m], wbuf[0, mine, :])
    swap.wait_recv()
    projected = projected + dot(conv[other], wbuf[0, theirs, :])
    hid[m] = (0.5 * projected * (1.0 + lax.erf(projected * math.sqrt(0.5)))).astype(BF16)
    swap = send(hid.at[m], hid.at[m], mp_s.at[1], mp_r.at[1], {"mp": other})
    for load in loads[1:]:
        load.wait()
    own = hid[m]
    raw_v = dot(own, wbuf[1, mine, :])
    raw_k = dot(own, wbuf[2, mine, :])
    raw_q = dot(own, wbuf[3, mine, :])
    swap.wait_recv()
    rest = hid[other]
    val[m] = (raw_v + dot(rest, wbuf[1, theirs, :])).astype(BF16)
    swap = send(val.at[m], val.at[m], mp_s.at[2], mp_r.at[2], {"mp": other})
    live_mask = lax.broadcasted_iota(jnp.int32, (rows, 1), 0) < live[0]

    def feature(x):
        x = jnp.where(x > 0.0, x + 1.0, jnp.exp(jnp.minimum(x, 0.0)))
        return jnp.where(live_mask, x, 0.0).astype(BF16)

    key_feat = feature(raw_k + dot(rest, wbuf[2, theirs, :]))
    key_wide = key_feat.astype(F32)
    key_t[...] = key_wide.T.astype(BF16)

    keep1 = pl.ds(pl.multiple_of(c * half, half), half)
    give1 = pl.ds(pl.multiple_of((1 - c) * half, half), half)
    keep2 = pl.ds(pl.multiple_of(y * quarter, quarter), quarter)
    give2 = pl.ds(pl.multiple_of((1 - y) * quarter, quarter), quarter)
    step1 = []

    def start1(g, column):
        send1[g] = dot(key_t[give1, :], val[column]).astype(BF16)
        step1.append(
            send(send1.at[g], recv1.at[g], s1_s.at[g], s1_r.at[g], {"parts": core_peer})
        )
        part[g] = dot(key_t[keep1, :], val[column])

    start1(0, m)
    query[...] = feature(raw_q + dot(rest, wbuf[3, theirs, :]))
    query_wide = query[...].astype(F32)
    lane = lax.broadcasted_iota(jnp.int32, (1, 128), 1)
    query_sq = jnp.sum(jnp.sum(query_wide * query_wide, axis=0, keepdims=True), axis=1, keepdims=True)
    key_sq = jnp.sum(jnp.sum(key_wide * key_wide, axis=0, keepdims=True), axis=1, keepdims=True)
    stat[0, :, :cols] = jnp.sum(key_wide, axis=0, keepdims=True)
    stat[0, :, cols:] = jnp.where(lane == 0, query_sq, jnp.where(lane == 1, key_sq, 0.0))
    swap.wait_recv()
    start1(1, other)
    stats = []
    for d in range(1, n):
        stats.append(
            send(stat.at[0], stat.at[d], st_s.at[d], st_r.at[d], {"parts": lax.rem(p + d, n)})
        )
    step2, step3 = {}, {}
    order = ((1, other), (0, m))
    for g, _ in order:
        step1[g].wait_recv()
        send2[g] = (
            part[g, give2, :]
            + recv1[g, give2, :].astype(F32)
        ).astype(BF16)
        step2[g] = send(
            send2.at[g], recv2.at[g], s2_s.at[g], s2_r.at[g], {"parts": y_peer}
        )
        acc2[g] = part[g, keep2, :] + recv1[g, keep2, :].astype(F32)
    for g, _ in order:
        step2[g].wait_recv()
        acc2[g] = acc2[g] + recv2[g].astype(F32)
        send3[g] = acc2[g].astype(BF16)
        for d in range(1, nz):
            to = lax.rem(z + d, nz)
            step3[g, d] = send(
                send3.at[g, pl.ds(pl.multiple_of(to * piece, piece), piece), :],
                recv3.at[g, d],
                s3_s.at[g, d],
                s3_r.at[g, d],
                {"parts": to * 4 + p % 4},
            )

    def block(column, yy, zz):
        first = c * half + yy * quarter + zz * piece
        return kvb.at[column, pl.ds(pl.multiple_of(first, piece), piece), :]

    gather_z, gather_y, gather_c = {}, {}, {}

    def to_core(g, place, i):
        gather_c[g, i] = send(
            place, place, gc_s.at[g, i], gc_r.at[g, i], {"parts": core_peer}
        )

    def pass_on(g, column, d):
        place = block(column, y, lax.rem(z + nz - d, nz))
        gather_y[g, d] = send(place, place, gy_s.at[g, d], gy_r.at[g, d], {"parts": y_peer})
        to_core(g, place, d)

    for g, column in order:
        final = acc2[g, pl.ds(pl.multiple_of(z * piece, piece), piece), :]
        for d in range(1, nz):
            step3[g, d].wait_recv()
            final = final + recv3[g, d].astype(F32)
        place = block(column, y, z)
        place[...] = final.astype(BF16)
        for d in range(1, nz):
            gather_z[g, d] = send(
                place,
                place,
                gz_s.at[g, d],
                gz_r.at[g, d],
                {"parts": lax.rem(z + d, nz) * 4 + p % 4},
            )
        pass_on(g, column, 0)

    for copy in stats:
        copy.wait_recv()
    sums = stat[0]
    for d in range(1, n):
        sums = sums + stat[d]
    den[m, :rows, :] = jnp.broadcast_to(
        jnp.sum(query_wide * sums[:, :cols], axis=1, keepdims=True), (rows, 128)
    )
    den[m, rows:, :] = jnp.broadcast_to(sums[:, cols:], (8, 128))
    den_swap = send(den.at[m], den.at[m], mp_s.at[3], mp_r.at[3], {"mp": other})

    for g, column in order:
        for d in range(1, nz):
            gather_z[g, d].wait_recv()
            pass_on(g, column, d)

    numerators = []
    for g, column in order:
        for d in range(nz):
            gather_y[g, d].wait_recv()
            to_core(g, block(column, 1 - y, lax.rem(z + nz - d, nz)), nz + d)
        for i in range(2 * nz):
            gather_c[g, i].wait_recv()
        numerators.append(dot(query[...], kvb[column]))
        if g == 1:
            nsend[...] = numerators[0].astype(BF16)
            swap = send(nsend, nrecv, mp_s.at[4], mp_r.at[4], {"mp": other})
    numerator = numerators[1]
    stores = []
    for g in range(2):
        store = pltpu.make_async_copy(kvb.at[g], kv_out.at[:, pl.ds(g * cols, cols)], osem.at[g])
        store.start()
        stores.append(store)
    den_swap.wait_recv()
    square = den[0, rows : rows + 1, :] + den[1, rows : rows + 1, :]
    query_sq = jnp.sum(jnp.where(lane == 0, square, 0.0), axis=1, keepdims=True)
    key_sq = jnp.sum(jnp.where(lane == 1, square, 0.0), axis=1, keepdims=True)
    inverse = lax.rsqrt(query_sq) * lax.rsqrt(key_sq)
    denominator = den[0, :rows, 0:1] + den[1, :rows, 0:1]
    scale = 1.0 + denominator * inverse
    swap.wait_recv()
    numerator = numerator + nrecv[...].astype(F32)
    result = (val[m].astype(F32) + numerator * inverse) / scale
    out[...] = jnp.where(live_mask, result, 0.0)
    for store in stores:
        store.wait()
    for copy in sent:
        copy.wait_send()


def fused(
    feats, adj_local, adj_halo, w_graph, w_query, w_key, w_value, send_rows, send_count, live
):
    n = lax.axis_size("parts")
    nz = n // 4
    rows, cols = feats.shape
    slots = send_rows.shape[2]
    depth = w_graph.shape[0]
    half, quarter, piece = cols // 2, cols // 4, cols // n
    vmem = pl.BlockSpec(memory_space=pltpu.VMEM)
    hbm = pl.BlockSpec(memory_space=pltpu.HBM)
    dma = pltpu.SemaphoreType.DMA
    place = functools.partial(pltpu.with_memory_space_constraint, memory_space=pltpu.HBM)
    out, kv = pl.pallas_call(
        functools.partial(kernel, n, nz),
        out_shape=(
            jax.ShapeDtypeStruct((rows, cols), F32),
            jax.ShapeDtypeStruct((cols, depth), BF16),
        ),
        in_specs=[hbm] * 5 + [pl.BlockSpec(memory_space=pltpu.SMEM)] + [hbm] * 4,
        out_specs=(vmem, pl.BlockSpec(memory_space=pl.ANY)),
        scratch_shapes=[
            pltpu.VMEM(feats.shape, BF16),
            pltpu.VMEM(adj_local.shape, BF16),
            pltpu.VMEM(adj_halo.shape, BF16),
            pltpu.VMEM((slots, n), jnp.int32),
            pltpu.VMEM((1, n), jnp.int32),
            pltpu.VMEM((4, depth, cols), BF16),
            pltpu.VMEM((n, slots, cols), BF16),
            pltpu.VMEM((n, slots, cols), BF16),
            pltpu.VMEM((2, rows, cols), BF16),
            pltpu.VMEM((2, rows, cols), BF16),
            pltpu.VMEM((2, rows, cols), BF16),
            pltpu.VMEM((rows, cols), BF16),
            pltpu.VMEM((cols, rows), BF16),
            pltpu.VMEM((2, half, cols), F32),
            pltpu.VMEM((2, half, cols), BF16),
            pltpu.VMEM((2, half, cols), BF16),
            pltpu.VMEM((2, quarter, cols), F32),
            pltpu.VMEM((2, quarter, cols), BF16),
            pltpu.VMEM((2, quarter, cols), BF16),
            pltpu.VMEM((2, quarter, cols), BF16),
            pltpu.VMEM((2, nz, piece, cols), BF16),
            pltpu.VMEM((2, cols, cols), BF16),
            pltpu.VMEM((n, 1, cols + 128), F32),
            pltpu.VMEM((2, rows + 8, 128), F32),
            pltpu.VMEM((rows, cols), BF16),
            pltpu.VMEM((rows, cols), BF16),
            dma((5,)),
            dma((4,)),
            dma((2,)),
            dma((n,)),
            dma((n,)),
            dma((5,)),
            dma((5,)),
            dma((2,)),
            dma((2,)),
            dma((2,)),
            dma((2,)),
            dma((2, nz)),
            dma((2, nz)),
            dma((2, nz)),
            dma((2, nz)),
            dma((2, nz)),
            dma((2, nz)),
            dma((2, 2 * nz)),
            dma((2, 2 * nz)),
            dma((n,)),
            dma((n,)),
        ],
        compiler_params=pltpu.CompilerParams(
            collective_id=0, has_side_effects=True, vmem_limit_bytes=24 * 1024 * 1024
        ),
    )(
        *(place(a) for a in (feats, adj_local, adj_halo, send_rows[0].T, send_count)),
        live,
        *(place(w) for w in (w_graph, w_query, w_key, w_value)),
    )
    return out, kv.astype(F32) / math.sqrt(n * rows)


def local(*args):
    n = lax.axis_size("parts")
    rows, cols = args[0].shape
    slots = args[7].shape[2]
    fits = (
        lax.axis_size("mp") == 2
        and n % 4 == 0
        and cols % (16 * n) == 0
        and rows % 16 == 0
        and (n * slots) % 16 == 0
        and slots % 8 == 0
    )
    return fused(*args) if fits else plain(*args)


def solution(mesh):
    return jax.shard_map(
        local,
        mesh=mesh,
        in_specs=(
            P("parts", "mp"),
            P("parts", None),
            P("parts", None),
            P(None, "mp"),
            P(None, "mp"),
            P(None, "mp"),
            P(None, "mp"),
            P("parts", None, None),
            P("parts", None),
            P("parts"),
        ),
        out_specs=(P("parts", "mp"), P("mp", None)),
        check_vma=False,
    )
```
